32 devices in a mesh: row: 16 (over z, y, x), col: 2 (over core).
Axes of the slice: x: 2, y: 2, z: 4, core: 2. Of those that a mesh axis runs over, the one named last changes fastest.
Arguments:
- environment: float32 [6144, 6144], P('row', 'col'), may hold values from -6 to 6
- site_tensors: float32 [2, 6144, 6144], P(None, 'row', 'col'), may hold values from -0.078125 to 0.078125
- panel_offset: int32 [1], replicated, may hold values from 0 to 6016
Outputs:
- new_panel: float32 [128, 6144], P('row', 'col')
The draws below stay inside these ranges and needn't reach their ends.
All inputs are finite; a program needn't handle non-finite values.
Results may differ from the reference program's by a relative error of at most 0.0001.
Values sent between devices are 32-bit elements; how exact they have to be, the bound alone decides.
A program may use at most 64 MiB of HBM per device.

```python
import jax
import jax.numpy as jnp
from jax import lax

D = 6144
PHYS = 2
PANEL = 128


def block_levels(key, extent, cuts, least, high):
    def one(position, parts):
        heights = jax.random.uniform(jax.random.fold_in(jax.random.fold_in(key, 6), position), (parts,), jnp.float32, least / len(cuts), high / len(cuts))
        return jnp.repeat(jnp.exp(heights), extent[position] // parts).reshape((-1,) + (1,) * (len(extent) - position - 1))

    loudness = one(*cuts[0])
    for cut in cuts[1:]:
        loudness = loudness * one(*cut)
    return loudness


def bell_draw(own_key, shape, width, limit, shards=(), held_as=jnp.bfloat16):
    values = jax.random.normal(own_key, shape, jnp.float32) * width
    if len(shards) > 0:
        values = block_levels(own_key, shape, shards, -0.22, 0.18) * values
    return jnp.clip(values, min=-limit, max=limit).astype(held_as)


def setup_inputs(seed: int = 0) -> dict:
    seeds = jax.random.split(jax.random.key(seed), 4)
    return {
        "environment": bell_draw(seeds[0], (D, D), 1.0, 6.0, ((0, 16), (1, 2)), jnp.float32),
        "site_tensors": bell_draw(seeds[1], (PHYS, D, D), D ** -0.5, 0.078125, ((1, 16), (2, 2)), jnp.float32),
        "panel_offset": jax.random.randint(seeds[2], (1,), 0, D - PANEL + 1).astype(jnp.int32),
    }


def reference(environment, site_tensors, panel_offset):
    result = jnp.zeros((PANEL, D), jnp.float32)
    for phys in range(PHYS):
        columns = lax.dynamic_slice_in_dim(site_tensors[phys], panel_offset[0].astype(jnp.int32), PANEL, 1)
        bond_block = jnp.dot(columns.T, environment, precision=lax.Precision.HIGHEST, preferred_element_type=jnp.float32)
        result = result + jnp.dot(bond_block, site_tensors[phys], precision=lax.Precision.HIGHEST, preferred_element_type=jnp.float32)
    return result
```

```python
import functools

import jax
import jax.numpy as jnp
from jax import lax
from jax.experimental import pallas as pl
from jax.experimental.pallas import tpu as pltpu
from jax.sharding import PartitionSpec as P

PHYS = 2
PANEL = 128
CHUNKS = 4
STRIPES = 2
F32 = jnp.float32
BF16 = jnp.bfloat16


def split(value):
    high = value.astype(BF16)
    return high, (value - high.astype(F32)).astype(BF16)


def dot3(lhs_high, lhs_low, rhs):
    high, low = split(rhs)
    dot = functools.partial(jnp.dot, preferred_element_type=F32)
    return dot(lhs_high, high) + (dot(lhs_high, low) + dot(lhs_low, high))


class Place:
    def __init__(self, rows, cols):
        row = lax.axis_index("row")
        self.col = lax.axis_index("col")
        self.rows, self.cols, self.depth = rows, cols, rows // 4
        self.x, self.y, self.z = row % 2, (row // 2) % 2, row // 4

    def at(self, x=None, y=None, z=None, col=None):
        x, y, z = (self.x if x is None else x), (self.y if y is None else y), (self.z if z is None else z)
        return (z * 4 + y * 2 + x, self.col if col is None else col)

    def other_z(self, j):
        return (self.z + j) % self.depth

    def other_col(self, j):
        return (self.col + j) % self.cols


def send(src, dst, send_sem, recv_sem, device):
    return pltpu.make_async_remote_copy(
        src_ref=src, dst_ref=dst, send_sem=send_sem, recv_sem=recv_sem, device_id=device, device_id_type=pl.DeviceIdType.MESH
    )


class Scatter:
    def __init__(self, place, base, parts, first, total, second, done, third, sems):
        self.place, self.base = place, base
        self.parts, self.first, self.total, self.second, self.done, self.third = parts, first, total, second, done, third
        self.sems = sems
        self.chunks, self.slots = parts.shape[1], parts.shape[2]

    @staticmethod
    def scratch(chunks, slots, depth, height, width):
        one = pltpu.VMEM((2, chunks, slots, height, width), F32)
        return [
            pltpu.VMEM((2, chunks, slots, 2, 2, height, width), F32),
            pltpu.VMEM((2, chunks, 2, slots, height, width), F32),
            one,
            one,
            one,
            pltpu.VMEM((2, chunks, depth, height, width), F32),
        ] + [
            pltpu.SemaphoreType.DMA(shape)
            for shape in [(2, chunks, 2)] * 2 + [(2, chunks)] * 2 + [(2, chunks, slots), (2, chunks, depth)]
        ]

    def one(self, half, k, last):
        here, sems = self.place, self.sems
        if half == 0:
            y, x, to = (here.y if last else 1 - here.y), 1 - here.x, here.at(x=1 - here.x)
        else:
            y, x, to = 1 - here.y, (here.x if last else 1 - here.x), here.at(y=1 - here.y)
        return send(
            self.parts.at[half, k, :, y, x], self.first.at[half, k, last], sems[0].at[half, k, last], sems[1].at[half, k, last], to
        )

    def two(self, half, k):
        here, sems = self.place, self.sems
        to = here.at(y=1 - here.y) if half == 0 else here.at(x=1 - here.x)
        return send(self.total.at[half, k], self.second.at[half, k], sems[2].at[half, k], sems[3].at[half, k], to)

    def three(self, half, k, slot, source):
        here, sems = self.place, self.sems
        return send(
            self.done.at[half, k, slot],
            self.third.at[half, k, source],
            sems[4].at[half, k, slot],
            sems[5].at[half, k, source],
            here.at(z=self.base + slot),
        )

    def start(self, half, k):
        self.one(half, k, 0).start()

    def middle(self):
        here = self.place

        def forward(k, carry):
            for half in range(2):
                self.one(half, k, 0).wait_recv()
                y, x = (1 - here.y, here.x) if half == 0 else (here.y, 1 - here.x)
                for slot in range(self.slots):
                    self.total[half, k, slot] = self.parts[half, k, slot, y, x] + self.first[half, k, 0, slot]
                self.two(half, k).start()
                self.one(half, k, 1).start()
            return carry

        lax.fori_loop(0, self.chunks, forward, 0)

        def across(k, carry):
            for half in range(2):
                self.one(half, k, 1).wait_recv()
                self.two(half, k).wait_recv()
                for slot in range(self.slots):
                    self.done[half, k, slot] = (
                        self.parts[half, k, slot, here.y, here.x] + self.first[half, k, 1, slot]
                    ) + self.second[half, k, slot]
                for slot in range(self.slots):

                    @pl.when(self.base + slot != here.z)
                    def _():
                        self.three(half, k, slot, here.z).start()

            return carry

        lax.fori_loop(0, self.chunks, across, 0)

    def result(self, half, k):
        here = self.place
        value = self.done[half, k, here.z - self.base]
        for j in range(1, here.depth):
            source = here.other_z(j)
            self.three(half, k, 0, source).wait_recv()
            value = value + self.third[half, k, source]
        return value

    def finish(self):
        here = self.place

        def drain(k, carry):
            for half in range(2):
                self.one(half, k, 0).wait_send()
                self.one(half, k, 1).wait_send()
                self.two(half, k).wait_send()
                for slot in range(self.slots):

                    @pl.when(self.base + slot != here.z)
                    def _():
                        self.three(half, k, slot, here.z).wait_send()

            return carry

        lax.fori_loop(0, self.chunks, drain, 0)


def kernel(rows, cols, window, env_hbm, site_hbm, out, env, site, windows, pan_high, pan_low, block, *rest):
    bond_refs, panel_refs, (load_sem, win_send, win_recv, block_send, block_recv) = rest[:12], rest[12:24], rest[24:]
    here = Place(rows, cols)
    env_load = pltpu.make_async_copy(env_hbm, env, load_sem.at[0])
    site_load = pltpu.make_async_copy(site_hbm, site, load_sem.at[1])
    env_load.start()
    site_load.start()

    barrier = pltpu.get_barrier_semaphore()
    partners = [here.at(x=1 - here.x), here.at(y=1 - here.y)]
    partners += [here.at(z=here.other_z(j)) for j in range(1, here.depth)]
    partners += [here.at(col=here.other_col(j)) for j in range(1, cols)]
    for partner in partners:
        pl.semaphore_signal(barrier, inc=1, device_id=partner, device_id_type=pl.DeviceIdType.MESH)
    pl.semaphore_wait(barrier, len(partners))

    def window_copy(j):
        return send(window, windows.at[j - 1], win_send.at[j - 1], win_recv.at[j - 1], here.at(col=here.other_col(j)))

    for j in range(1, cols):
        window_copy(j).start()
    for j in range(1, cols):
        window_copy(j).wait_recv()
    for phys in range(PHYS):
        columns = window[phys]
        for j in range(1, cols):
            columns = columns + windows[j - 1, phys]
        high, low = split(columns.T)
        pan_high[pl.ds(phys * PANEL, PANEL), :] = high
        pan_low[pl.ds(phys * PANEL, PANEL), :] = low

    depth_local = env.shape[0]
    slots = bond_refs[0].shape[2]
    owner = here.z // slots
    bond = Scatter(here, here.col * slots, *bond_refs[:6], bond_refs[6:])
    env_load.wait()

    def partial_blocks(y, x):
        def one(slot, carry):
            offset = pl.multiple_of((slot * 4 + y * 2 + x) * depth_local, 128)
            product = dot3(pan_high[...], pan_low[...], env[:, pl.ds(offset, depth_local)])
            product = product.reshape(PHYS, CHUNKS, PANEL // CHUNKS, depth_local)
            for phys in range(PHYS):
                for k in range(CHUNKS):
                    bond.parts[phys, k, slot, y, x] = product[phys, k]
            return carry

        lax.fori_loop(0, slots, one, 0)

    partial_blocks(1 - here.y, 1 - here.x)
    for k in range(CHUNKS):
        bond.start(0, k)
        bond.start(1, k)
    partial_blocks(1 - here.y, here.x)
    partial_blocks(here.y, 1 - here.x)
    partial_blocks(here.y, here.x)
    bond.middle()

    def block_copy(half, k, j):
        return send(
            block.at[half, k],
            block.at[half, k],
            block_send.at[half, k, j - 1],
            block_recv.at[half, k],
            here.at(col=here.other_col(j)),
        )

    @pl.when(owner == here.col)
    def _():
        def own(k, carry):
            for half in range(2):
                block[half, k] = bond.result(half, k)
                for j in range(1, cols):
                    block_copy(half, k, j).start()
            return carry

        lax.fori_loop(0, CHUNKS, own, 0)

    @pl.when(owner != here.col)
    def _():
        def fetch(k, carry):
            for half in range(2):
                block_copy(half, k, 1).wait_recv()
            return carry

        lax.fori_loop(0, CHUNKS, fetch, 0)

    panel = Scatter(here, 0, *panel_refs[:6], panel_refs[6:])
    site_load.wait()
    lhs = [split(block[phys].reshape(PANEL, depth_local)) for phys in range(PHYS)]
    width = panel.parts.shape[-1]
    height = panel.parts.shape[-2]
    for k in range(STRIPES):
        for half in range(2):
            columns = pl.ds((half * STRIPES + k) * width, width)
            product = dot3(*lhs[0], site[0, :, columns])
            for phys in range(1, PHYS):
                product = product + dot3(*lhs[phys], site[phys, :, columns])
            panel.parts[half, k] = product.reshape(here.depth, 2, 2, height, width)
            panel.start(half, k)
    panel.middle()
    for k in range(STRIPES):
        for half in range(2):
            out[:, pl.ds((half * STRIPES + k) * width, width)] = panel.result(half, k)

    for j in range(1, cols):
        window_copy(j).wait_send()

    @pl.when(owner == here.col)
    def _():
        def own_drain(k, carry):
            for half in range(2):
                for j in range(1, cols):
                    block_copy(half, k, j).wait_send()
            return carry

        lax.fori_loop(0, CHUNKS, own_drain, 0)

    bond.finish()
    panel.finish()


def panel_window(site_tensors, panel_offset):
    cols_local = site_tensors.shape[2]
    padded = jnp.pad(site_tensors, ((0, 0), (0, 0), (PANEL, PANEL)))
    slice_start = jnp.clip(panel_offset[0] - lax.axis_index("col") * cols_local + PANEL, 0, cols_local + PANEL)
    return lax.dynamic_slice_in_dim(padded, slice_start, PANEL, 2)


def one_kernel(rows, cols, environment, site_tensors, panel_offset):
    depth_local, cols_local = environment.shape
    slots = cols_local // depth_local // 4
    depth = rows // 4
    height = PANEL // CHUNKS
    any_space = pl.BlockSpec(memory_space=pl.ANY)
    in_vmem = pl.BlockSpec(memory_space=pltpu.VMEM)
    return pl.pallas_call(
        functools.partial(kernel, rows, cols),
        out_shape=jax.ShapeDtypeStruct((PANEL // rows, cols_local), F32),
        in_specs=[in_vmem, any_space, any_space],
        out_specs=in_vmem,
        scratch_shapes=[
            pltpu.VMEM(environment.shape, F32),
            pltpu.VMEM(site_tensors.shape, F32),
            pltpu.VMEM((cols - 1, PHYS, depth_local, PANEL), F32),
            pltpu.VMEM((PHYS * PANEL, depth_local), BF16),
            pltpu.VMEM((PHYS * PANEL, depth_local), BF16),
            pltpu.VMEM((PHYS, CHUNKS, height, depth_local), F32),
        ]
        + Scatter.scratch(CHUNKS, slots, depth, height, depth_local)
        + Scatter.scratch(STRIPES, depth, depth, PANEL // rows, cols_local // (2 * STRIPES))
        + [
            pltpu.SemaphoreType.DMA((2,)),
            pltpu.SemaphoreType.DMA((cols - 1,)),
            pltpu.SemaphoreType.DMA((cols - 1,)),
            pltpu.SemaphoreType.DMA((2, CHUNKS, cols - 1)),
            pltpu.SemaphoreType.DMA((2, CHUNKS)),
        ],
        compiler_params=pltpu.CompilerParams(collective_id=0, has_side_effects=True, vmem_limit_bytes=60 * 1024 * 1024),
    )(panel_window(site_tensors, panel_offset), environment, site_tensors)


def collectives(environment, site_tensors, panel_offset):
    rows_local, cols_local = environment.shape
    col_index = lax.axis_index("col")
    panel_rows = lax.psum(panel_window(site_tensors, panel_offset), "col")
    first_col = lax.axis_index("row") * rows_local
    owner_col = first_col // cols_local
    owner_mask = (col_index == owner_col).astype(F32)
    accumulated = jnp.zeros((PANEL, cols_local), F32)
    for phys in range(PHYS):
        partial_one = jnp.dot(
            panel_rows[phys].T, environment, precision=lax.Precision.HIGHEST, preferred_element_type=F32
        )
        block_one = lax.dynamic_slice_in_dim(lax.psum(partial_one, "row"), first_col - owner_col * cols_local, rows_local, 1)
        fetched_one = lax.psum(block_one * owner_mask, "col")
        accumulated = accumulated + jnp.dot(
            fetched_one, site_tensors[phys], precision=lax.Precision.HIGHEST, preferred_element_type=F32
        )
    return lax.psum_scatter(accumulated, "row", scatter_dimension=0, tiled=True)


def solution(mesh):
    rows, cols = mesh.shape["row"], mesh.shape["col"]

    def shards(environment, site_tensors, panel_offset):
        depth_local, cols_local = environment.shape
        fits = (
            rows % 8 == 0
            and cols > 1
            and depth_local % 128 == 0
            and cols_local % (4 * depth_local) == 0
            and cols_local % (2 * STRIPES * 128) == 0
            and PANEL % (8 * rows) == 0
            and rows * depth_local == cols * cols_local
        )
        if fits:
            return one_kernel(rows, cols, environment, site_tensors, panel_offset)
        return collectives(environment, site_tensors, panel_offset)

    return jax.shard_map(
        shards,
        mesh=mesh,
        in_specs=(P("row", "col"), P(None, "row", "col"), P()),
        out_specs=P("row", "col"),
        check_vma=False,
    )
```

```python
import functools

import jax
import jax.numpy as jnp
from jax import lax
from jax.experimental import pallas as pl
from jax.experimental.pallas import tpu as pltpu
from jax.sharding import PartitionSpec as P

PHYS = 2
PANEL = 128
GROUPS = 2
STRIPES = 2
F32 = jnp.float32
BF16 = jnp.bfloat16


def split(value):
    high = value.astype(BF16)
    return high, (value - high.astype(F32)).astype(BF16)


def stacked(value):
    return jnp.concatenate(split(value), axis=0)


def dot3(lhs, rhs_high, rhs_low):
    count = lhs.shape[0] // 2
    dot = functools.partial(jnp.dot, preferred_element_type=F32)
    both = dot(lhs, rhs_high)
    return both[:count] + (both[count:] + dot(lhs[:count], rhs_low))


def z_order(depth):
    return sorted(range(depth), key=lambda z: (-abs(2 * z - depth + 1), z))


class Place:
    def __init__(self, rows, cols):
        row = lax.axis_index("row")
        self.col = lax.axis_index("col")
        self.rows, self.cols, self.depth = rows, cols, rows // 4
        self.x, self.y, self.z = row % 2, (row // 2) % 2, row // 4

    def at(self, x=None, y=None, z=None, col=None):
        x, y, z = (self.x if x is None else x), (self.y if y is None else y), (self.z if z is None else z)
        return (z * 4 + y * 2 + x, self.col if col is None else col)

    def other_z(self, j):
        return (self.z + j) % self.depth

    def other_col(self, j):
        return (self.col + j) % self.cols


def send(src, dst, send_sem, recv_sem, device):
    return pltpu.make_async_remote_copy(
        src_ref=src, dst_ref=dst, send_sem=send_sem, recv_sem=recv_sem, device_id=device, device_id_type=pl.DeviceIdType.MESH
    )


class Scatter:
    def __init__(self, place, dest, parts, first, total, second, done, third, sems):
        self.place, self.dest = place, dest
        self.parts, self.first, self.total, self.second, self.done, self.third = parts, first, total, second, done, third
        self.sems = sems
        self.chunks, self.slots = parts.shape[1], parts.shape[2]

    @staticmethod
    def scratch(chunks, slots, depth, height, width):
        one = pltpu.VMEM((2, chunks, slots, height, width), F32)
        return [
            pltpu.VMEM((2, chunks, slots, 2, 2, height, width), F32),
            pltpu.VMEM((2, chunks, 2, slots, height, width), F32),
            one,
            one,
            one,
            pltpu.VMEM((2, chunks, depth, height, width), F32),
        ] + [
            pltpu.SemaphoreType.DMA(shape)
            for shape in [(2, chunks, 2)] * 2 + [(2, chunks)] * 2 + [(2, chunks, slots), (2, chunks, depth)]
        ]

    def one(self, half, k, last):
        here, sems = self.place, self.sems
        if half == 0:
            y, x, to = (here.y if last else 1 - here.y), 1 - here.x, here.at(x=1 - here.x)
        else:
            y, x, to = 1 - here.y, (here.x if last else 1 - here.x), here.at(y=1 - here.y)
        return send(
            self.parts.at[half, k, :, y, x], self.first.at[half, k, last], sems[0].at[half, k, last], sems[1].at[half, k, last], to
        )

    def two(self, half, k):
        here, sems = self.place, self.sems
        to = here.at(y=1 - here.y) if half == 0 else here.at(x=1 - here.x)
        return send(self.total.at[half, k], self.second.at[half, k], sems[2].at[half, k], sems[3].at[half, k], to)

    def three(self, half, k, slot, source):
        here, sems = self.place, self.sems
        return send(
            self.done.at[half, k, slot],
            self.third.at[half, k, source],
            sems[4].at[half, k, slot],
            sems[5].at[half, k, source],
            here.at(z=self.dest[slot]),
        )

    def start(self, half, k):
        self.one(half, k, 0).start()

    def forward(self, k):
        here = self.place
        for half in range(2):
            self.one(half, k, 0).wait_recv()
            y, x = (1 - here.y, here.x) if half == 0 else (here.y, 1 - here.x)
            for slot in range(self.slots):
                self.total[half, k, slot] = self.parts[half, k, slot, y, x] + self.first[half, k, 0, slot]
            self.two(half, k).start()
            self.one(half, k, 1).start()

    def across(self, k):
        here = self.place
        for half in range(2):
            self.one(half, k, 1).wait_recv()
            self.two(half, k).wait_recv()
            for slot in range(self.slots):
                self.done[half, k, slot] = (
                    self.parts[half, k, slot, here.y, here.x] + self.first[half, k, 1, slot]
                ) + self.second[half, k, slot]
            for slot in range(self.slots):

                @pl.when(self.dest[slot] != here.z)
                def _():
                    self.three(half, k, slot, here.z).start()

    def result(self, half, k, slot):
        here = self.place
        value = self.done[half, k, slot]
        for j in range(1, here.depth):
            source = here.other_z(j)
            self.three(half, k, slot, source).wait_recv()
            value = value + self.third[half, k, source]
        return value

    def finish(self):
        here = self.place

        def drain(k, carry):
            for half in range(2):
                self.one(half, k, 0).wait_send()
                self.one(half, k, 1).wait_send()
                self.two(half, k).wait_send()
                for slot in range(self.slots):

                    @pl.when(self.dest[slot] != here.z)
                    def _():
                        self.three(half, k, slot, here.z).wait_send()

            return carry

        lax.fori_loop(0, self.chunks, drain, 0)


def kernel(rows, cols, window, env_hbm, site_hbm, out, env, site, high_env, low_env, high_site, low_site, windows, pan, block, *rest):
    load_sem, win_send, win_recv, block_send, block_recv = rest[:5]
    bond_refs, panel_refs = rest[5:17], [rest[17 + 12 * g : 29 + 12 * g] for g in range(GROUPS)]
    here = Place(rows, cols)
    env_load = pltpu.make_async_copy(env_hbm, env, load_sem.at[0])
    site_load = pltpu.make_async_copy(site_hbm, site, load_sem.at[1])
    env_load.start()
    site_load.start()

    barrier = pltpu.get_barrier_semaphore()
    partners = [here.at(x=1 - here.x), here.at(y=1 - here.y)]
    partners += [here.at(z=here.other_z(j)) for j in range(1, here.depth)]
    partners += [here.at(col=here.other_col(j)) for j in range(1, cols)]
    for partner in partners:
        pl.semaphore_signal(barrier, inc=1, device_id=partner, device_id_type=pl.DeviceIdType.MESH)
    depth_local, cols_local = env.shape
    step = 16
    env_load.wait()

    def split_env(i, carry):
        at = pl.ds(pl.multiple_of(i * step, step), step)
        high_env[at, :], low_env[at, :] = split(env[at, :])
        return carry

    lax.fori_loop(0, depth_local // step, split_env, 0)
    pl.semaphore_wait(barrier, len(partners))

    def window_copy(j):
        return send(window, windows.at[j - 1], win_send.at[j - 1], win_recv.at[j - 1], here.at(col=here.other_col(j)))

    for j in range(1, cols):
        window_copy(j).start()
    for j in range(1, cols):
        window_copy(j).wait_recv()
    order = z_order(here.depth)
    height = PANEL // here.depth
    for phys in range(PHYS):
        columns = window[phys]
        for j in range(1, cols):
            columns = columns + windows[j - 1, phys]
        flipped = columns.T
        for k, z in enumerate(order):
            at = phys * PANEL + k * height
            high, low = split(flipped[z * height : (z + 1) * height])
            pan[at : at + height, :] = high
            pan[PHYS * PANEL + at : PHYS * PANEL + at + height, :] = low

    slots = bond_refs[0].shape[2]
    bond = Scatter(here, [here.col * slots + slot for slot in range(slots)], *bond_refs[:6], bond_refs[6:])

    def partial_blocks(y, x):
        def one(slot, carry):
            columns = pl.ds(pl.multiple_of((slot * 4 + y * 2 + x) * depth_local, 128), depth_local)
            product = dot3(pan[...], high_env[:, columns], low_env[:, columns])
            product = product.reshape(PHYS, here.depth, height, depth_local)
            for phys in range(PHYS):
                for k in range(here.depth):
                    bond.parts[phys, k, slot, y, x] = product[phys, k]
            return carry

        lax.fori_loop(0, slots, one, 0)

    each = here.depth // GROUPS

    def members(g):
        return range(g * each, (g + 1) * each)

    def start_bond(g):
        for k in members(g):
            bond.start(0, k)
            bond.start(1, k)

    def block_copy(half, k, j):
        to = here.at(col=here.other_col(j))
        return send(
            block.at[half, k], block.at[half, k], block_send.at[half, k, j - 1], block_recv.at[half, k], to
        )

    def share_block(k):
        for slot in range(slots):

            @pl.when(bond.dest[slot] == here.z)
            def _():
                for half in range(2):
                    block[half, k] = bond.result(half, k, slot)
                    for j in range(1, cols):
                        block_copy(half, k, j).start()

    def fetch_block(k):
        @pl.when(here.z // slots != here.col)
        def _():
            for half in range(2):
                block_copy(half, k, 1).wait_recv()

    panels = [
        Scatter(here, [order[k] for k in members(g)], *panel_refs[g][:6], panel_refs[g][6:]) for g in range(GROUPS)
    ]
    width = panels[0].parts.shape[-1]

    def split_site(i, carry):
        at = pl.ds(pl.multiple_of(i * step, step), step)
        for phys in range(PHYS):
            to = pl.ds(pl.multiple_of(phys * depth_local + i * step, step), step)
            high_site[to, :], low_site[to, :] = split(site[phys, at, :])
        return carry

    def start_panel(g):
        rows_of = [block[phys, g * each : (g + 1) * each].reshape(each * height, depth_local) for phys in range(PHYS)]
        lhs = stacked(jnp.concatenate(rows_of, axis=1))
        for k in range(STRIPES):
            for half in range(2):
                columns = pl.ds((half * STRIPES + k) * width, width)
                product = dot3(lhs, high_site[:, columns], low_site[:, columns])
                panels[g].parts[half, k] = product.reshape(panels[g].parts.shape[2:])
                panels[g].start(half, k)

    def finish_panel(g):
        for slot in range(each):

            @pl.when(panels[g].dest[slot] == here.z)
            def _():
                for k in range(STRIPES):
                    for half in range(2):
                        out[:, pl.ds((half * STRIPES + k) * width, width)] = panels[g].result(half, k, slot)

    partial_blocks(1 - here.y, 1 - here.x)
    start_bond(0)
    partial_blocks(1 - here.y, here.x)
    partial_blocks(here.y, 1 - here.x)
    partial_blocks(here.y, here.x)
    site_load.wait()
    lax.fori_loop(0, depth_local // step, split_site, 0)
    for g in range(GROUPS):
        for k in members(g):
            bond.forward(k)
        if g + 1 < GROUPS:
            start_bond(g + 1)
        if g > 0:
            for k in members(g - 1):
                fetch_block(k)
            start_panel(g - 1)
        for k in members(g):
            bond.across(k)
        if g > 0:
            for k in range(STRIPES):
                panels[g - 1].forward(k)
        for k in members(g):
            share_block(k)
        if g > 0:
            for k in range(STRIPES):
                panels[g - 1].across(k)
    for k in members(GROUPS - 1):
        fetch_block(k)
    start_panel(GROUPS - 1)
    for k in range(STRIPES):
        panels[-1].forward(k)
    for g in range(GROUPS - 1):
        finish_panel(g)
    for k in range(STRIPES):
        panels[-1].across(k)
    finish_panel(GROUPS - 1)

    for j in range(1, cols):
        window_copy(j).wait_send()

    @pl.when(here.z // slots == here.col)
    def _():
        def drain(k, carry):
            for half in range(2):
                for j in range(1, cols):
                    block_copy(half, k, j).wait_send()
            return carry

        lax.fori_loop(0, here.depth, drain, 0)

    bond.finish()
    for panel in panels:
        panel.finish()


def panel_window(site_tensors, panel_offset):
    cols_local = site_tensors.shape[2]
    padded = jnp.pad(site_tensors, ((0, 0), (0, 0), (PANEL, PANEL)))
    slice_start = jnp.clip(panel_offset[0] - lax.axis_index("col") * cols_local + PANEL, 0, cols_local + PANEL)
    return lax.dynamic_slice_in_dim(padded, slice_start, PANEL, 2)


def one_kernel(rows, cols, environment, site_tensors, panel_offset):
    depth_local, cols_local = environment.shape
    slots = cols_local // depth_local // 4
    depth = rows // 4
    height = PANEL // depth
    any_space = pl.BlockSpec(memory_space=pl.ANY)
    in_vmem = pl.BlockSpec(memory_space=pltpu.VMEM)
    return pl.pallas_call(
        functools.partial(kernel, rows, cols),
        out_shape=jax.ShapeDtypeStruct((PANEL // rows, cols_local), F32),
        in_specs=[in_vmem, any_space, any_space],
        out_specs=in_vmem,
        scratch_shapes=[
            pltpu.VMEM(environment.shape, F32),
            pltpu.VMEM(site_tensors.shape, F32),
            pltpu.VMEM(environment.shape, BF16),
            pltpu.VMEM(environment.shape, BF16),
            pltpu.VMEM((PHYS * depth_local, cols_local), BF16),
            pltpu.VMEM((PHYS * depth_local, cols_local), BF16),
            pltpu.VMEM((cols - 1, PHYS, depth_local, PANEL), F32),
            pltpu.VMEM((2 * PHYS * PANEL, depth_local), BF16),
            pltpu.VMEM((PHYS, depth, height, depth_local), F32),
            pltpu.SemaphoreType.DMA((2,)),
            pltpu.SemaphoreType.DMA((cols - 1,)),
            pltpu.SemaphoreType.DMA((cols - 1,)),
            pltpu.SemaphoreType.DMA((2, depth, cols - 1)),
            pltpu.SemaphoreType.DMA((2, depth)),
        ]
        + Scatter.scratch(depth, slots, depth, height, depth_local)
        + GROUPS * Scatter.scratch(STRIPES, depth // GROUPS, depth, PANEL // rows, cols_local // (2 * STRIPES)),
        compiler_params=pltpu.CompilerParams(collective_id=0, has_side_effects=True, vmem_limit_bytes=60 * 1024 * 1024),
    )(panel_window(site_tensors, panel_offset), environment, site_tensors)


def collectives(environment, site_tensors, panel_offset):
    rows_local, cols_local = environment.shape
    col_index = lax.axis_index("col")
    panel_rows = lax.psum(panel_window(site_tensors, panel_offset), "col")
    first_col = lax.axis_index("row") * rows_local
    owner_col = first_col // cols_local
    owner_mask = (col_index == owner_col).astype(F32)
    accumulated = jnp.zeros((PANEL, cols_local), F32)
    for phys in range(PHYS):
        partial_one = jnp.dot(
            panel_rows[phys].T, environment, precision=lax.Precision.HIGHEST, preferred_element_type=F32
        )
        block_one = lax.dynamic_slice_in_dim(lax.psum(partial_one, "row"), first_col - owner_col * cols_local, rows_local, 1)
        fetched_one = lax.psum(block_one * owner_mask, "col")
        accumulated = accumulated + jnp.dot(
            fetched_one, site_tensors[phys], precision=lax.Precision.HIGHEST, preferred_element_type=F32
        )
    return lax.psum_scatter(accumulated, "row", scatter_dimension=0, tiled=True)


def solution(mesh):
    rows, cols = mesh.shape["row"], mesh.shape["col"]

    def shards(environment, site_tensors, panel_offset):
        depth_local, cols_local = environment.shape
        fits = (
            rows % (4 * GROUPS) == 0
            and cols > 1
            and depth_local % 128 == 0
            and cols_local % (4 * depth_local) == 0
            and cols_local % (2 * STRIPES * 128) == 0
            and PANEL % (8 * rows) == 0
            and rows * depth_local == cols * cols_local
        )
        if fits:
            return one_kernel(rows, cols, environment, site_tensors, panel_offset)
        return collectives(environment, site_tensors, panel_offset)

    return jax.shard_map(
        shards,
        mesh=mesh,
        in_specs=(P("row", "col"), P(None, "row", "col"), P()),
        out_specs=P("row", "col"),
        check_vma=False,
    )
```
